128 devices in a mesh: row: 16 (over z_hi, x, core), col: 8 (over z_lo, y).
Axes of the slice: x: 4, y: 4, z: 4 (z_hi: 2, z_lo: 2; z = z_hi * 2 + z_lo), core: 2. Of those that a mesh axis runs over, the one named last changes fastest.
Arguments:
- integrals: bfloat16 [6144, 6144], P('row', 'col'), may hold values from -0.078125 to 0.078125
- amplitudes: bfloat16 [6144, 12288], P('row', 'col'), may hold values from -6 to 6
- tile_pattern: int32 [48, 48], replicated, may hold values 0 or 1
- pair_domain: int32 [48, 12288], P(None, 'col'), may hold values 0 or 1
- tile_order: int32 [48], replicated, may hold values from 0 to 47, each once
Outputs:
- ladder: float32 [6144, 12288], P('row', 'col')
The draws below stay inside these ranges and needn't reach their ends.
Inputs may be any that keep to these rules, and one draw needn't show every extreme that they name: tile_order holds each tile number once.
All inputs are finite; a program needn't handle non-finite values. No bound on the sum of `pair_domain` on one device may be relied on, other than what follows from the above.
Results may differ from the reference program's by a relative error of at most 0.0003.
Values may be sent and summed in bfloat16 or wider, within the bound.
No kernel may reach another device: no remote copies, remote signals or barrier semaphores. Data moves between devices by JAX's collectives and lax.ppermute only.
A program may use at most 128 MiB of HBM per device.

```python
import jax
import jax.numpy as jnp
from jax import lax

V = 6144
TILE = 128
TILES = 48
PAIRS = 12288


def plant(values, rng, smallest, top_value):
    dims = values.shape
    place = [jax.random.randint(jax.random.fold_in(rng, axis), (), 0, dims[axis]) for axis in range(len(dims))]
    values = values.at[tuple(place)].set(smallest)
    longest = dims.index(max(dims))
    place[longest] = (place[longest] + 1) % dims[longest]
    return values.at[tuple(place)].set(top_value)


def level_of(stream_key, dims, shards, low, largest):
    gain, own = 1.0, jax.random.fold_in(stream_key, 6)
    for position, blocks in shards:
        draws = jnp.exp(jax.random.uniform(jax.random.fold_in(own, position), (blocks,), jnp.float32, low / len(shards), largest / len(shards)))
        gain = gain * jnp.repeat(draws, dims[position] // blocks).reshape([-1 if axis == position else 1 for axis in range(len(dims))])
    return gain


def normal_values(stream_key, dims, width, most, cuts=(), kind=jnp.bfloat16):
    loudness = level_of(stream_key, dims, cuts, -0.22, 0.18) if cuts else 1.0
    drawn = jax.random.normal(stream_key, dims, jnp.float32) * width * loudness
    return jnp.minimum(jnp.maximum(drawn, -most), most).astype(kind)


def setup_inputs(seed: int = 0) -> dict:
    seeds = jax.random.split(jax.random.key(seed), 6)
    return {
        "integrals": normal_values(seeds[0], (V, V), V ** -0.5, 0.078125, ((0, 16), (1, 8))),
        "amplitudes": normal_values(seeds[1], (V, PAIRS), 1.0, 6.0, ((0, 16), (1, 8))),
        "tile_pattern": plant((jax.random.randint(seeds[2], (TILES, TILES), 0, 4) < 3).astype(jnp.int32), jax.random.fold_in(seeds[2], 1), 0, 1),
        "pair_domain": plant((jax.random.randint(seeds[3], (TILES, PAIRS), 0, 2) < 1).astype(jnp.int32), jax.random.fold_in(seeds[3], 1), 0, 1),
        "tile_order": jax.random.permutation(seeds[4], TILES).astype(jnp.int32),
    }


def storage_masks(tile_pattern, pair_domain, tile_order):
    count = tile_order.shape[0]
    placed = (tile_order[:, None] == jnp.arange(count, dtype=jnp.int32)[None, :]).astype(jnp.float32)
    pattern_stored = jnp.dot(jnp.dot(placed, tile_pattern.astype(jnp.float32), precision=lax.Precision.HIGHEST), placed.T, precision=lax.Precision.HIGHEST)
    domain_stored = jnp.dot(placed, pair_domain.astype(jnp.float32), precision=lax.Precision.HIGHEST)
    return pattern_stored, domain_stored


def reference(integrals, amplitudes, tile_pattern, pair_domain, tile_order):
    pattern_stored, domain_stored = storage_masks(tile_pattern, pair_domain, tile_order)
    integral_mask = jnp.repeat(jnp.repeat(pattern_stored, TILE, axis=0), TILE, axis=1).astype(jnp.bfloat16)
    domain_mask = jnp.repeat(domain_stored, TILE, axis=0).astype(jnp.bfloat16)
    screened = integrals * integral_mask
    restricted = amplitudes * domain_mask
    return jnp.dot(screened, restricted, preferred_element_type=jnp.float32)
```

```python
import functools

import jax
import jax.numpy as jnp
import numpy as np
from jax import lax
from jax.experimental import pallas as pl
from jax.experimental.pallas import tpu as pltpu
from jax.sharding import Mesh, PartitionSpec as P

TILE = 128
AXES = ("zh", "x", "core", "zl", "y")
SIZES = (2, 4, 2, 2, 4)
ROW, COL = ("zh", "x", "core"), ("zl", "y")
BF16, F32, I32 = jnp.bfloat16, jnp.float32, jnp.int32
FLAG_ROWS = 8
VMEM_LIMIT = 60 << 20


def iota(shape, dim):
    return lax.broadcasted_iota(I32, shape, dim)


def whole(n, space=pltpu.VMEM):
    return [pl.BlockSpec(memory_space=space)] * n


def plan_kernel(tall, slots, order, pattern, place, a_ref, d_ref, keep_ref, send_ref, pos_ref, start_ref, dom):
    row, col, core = place[0], place[1], place[2]
    tiles, pairs = d_ref.shape
    rows, cols = a_ref.shape
    half = cols // TILE // 2
    for s in range(tiles):
        dom[pl.ds(s, 1), :] = d_ref[pl.ds(order[s], 1), :]
    live = dom[...].astype(F32).astype(BF16)
    blocks = pairs // TILE
    spread = (iota((pairs, TILE), 0) // TILE == iota((pairs, TILE), 1)).astype(F32).astype(BF16)
    counts = jnp.dot(live, spread, preferred_element_type=F32)
    below = (iota((TILE, TILE), 0) < iota((TILE, TILE), 1)).astype(F32).astype(BF16)
    upto = (iota((TILE, TILE), 0) <= iota((TILE, TILE), 1)).astype(F32).astype(BF16)
    s0, s1 = iota((tiles, tiles), 0), iota((tiles, tiles), 1)
    before = ((s0 // tall == s1 // tall) & (s1 < s0)).astype(F32).astype(BF16)
    counted = counts.astype(BF16)
    ahead = jnp.sum(jnp.dot(before, counted, preferred_element_type=F32), axis=1, keepdims=True)
    starts = jnp.dot(counted, below, preferred_element_type=F32) + ahead
    start_ref[...] = starts.astype(I32)
    for b in range(blocks):
        lanes = pl.ds(b * TILE, TILE)
        here = live[:, b * TILE : (b + 1) * TILE]
        slot = jnp.dot(here, upto, preferred_element_type=F32) + (starts[:, b : b + 1] - 1.0)
        pos_ref[:, lanes] = jnp.where(dom[:, lanes] > 0, slot.astype(I32), -1)
    most = jnp.max(ahead + jnp.sum(counts, axis=1, keepdims=True), axis=0, keepdims=True)
    flag = jnp.where(most > slots, 1.0, 0.0).astype(F32)
    keep_ref[pl.ds(rows, FLAG_ROWS), :] = jnp.broadcast_to(flag, (FLAG_ROWS, cols // 2)).astype(BF16)
    for i in range(rows // TILE):
        high = pl.ds(i * TILE, TILE)
        for j in range(half):
            for ref, base in ((keep_ref, core * half), (send_ref, (1 - core) * half)):
                tile = base + j
                on = pattern[order[row * tall + i], order[col * 2 * half + tile]]
                scale = on.astype(F32).astype(BF16)
                part = a_ref[high, pl.ds(pl.multiple_of(tile * TILE, TILE), TILE)]
                ref[high, pl.ds(j * TILE, TILE)] = part * scale


def plan(integrals, tile_pattern, pair_domain, tile_order, place, tall, slots):
    rows, cols = integrals.shape
    tiles, pairs = pair_domain.shape
    return pl.pallas_call(
        functools.partial(plan_kernel, tall, slots),
        grid_spec=pltpu.PrefetchScalarGridSpec(
            num_scalar_prefetch=3,
            grid=(),
            in_specs=whole(2),
            out_specs=whole(4),
            scratch_shapes=[pltpu.VMEM((tiles, pairs), I32)],
        ),
        out_shape=[
            jax.ShapeDtypeStruct((rows + FLAG_ROWS, cols // 2), BF16),
            jax.ShapeDtypeStruct((rows, cols // 2), BF16),
            jax.ShapeDtypeStruct((tiles, pairs), I32),
            jax.ShapeDtypeStruct((tiles, TILE), I32),
        ],
        name="plan",
    )(tile_order, tile_pattern, place, integrals, pair_domain)


def compact_kernel(slots, start, place, b_ref, pos_ref, u_ref, f_ref, g_ref, total):
    tall = b_ref.shape[0] // TILE
    total[...] = jnp.zeros_like(total)
    for i in range(tall):
        s = place[0] * tall + i
        slot = pos_ref[pl.ds(s, 1), :]
        for b in range(b_ref.shape[1] // TILE):
            lanes = pl.ds(b * TILE, TILE)
            at = jnp.minimum(start[s, b] // TILE * TILE, slots)
            at = pl.multiple_of(at, TILE)
            pick = (iota((2 * TILE, TILE), 0) + at == slot[:, b * TILE : (b + 1) * TILE]).astype(F32).astype(BF16)
            moved = lax.dot_general(
                b_ref[pl.ds(i * TILE, TILE), lanes], pick, (((1,), (1,)), ((), ())), preferred_element_type=F32
            )
            total[:, pl.ds(at, 2 * TILE)] += moved
    packed = total[:, :slots].astype(BF16)
    first = f_ref.shape[0]
    u_ref[...] = packed
    f_ref[...] = packed[:first]
    g_ref[...] = packed[first:]


def compact(start, place, amplitudes, pos, slots, first):
    return pl.pallas_call(
        functools.partial(compact_kernel, slots),
        grid_spec=pltpu.PrefetchScalarGridSpec(
            num_scalar_prefetch=2,
            grid=(),
            in_specs=whole(2),
            out_specs=whole(3),
            scratch_shapes=[pltpu.VMEM((TILE, slots + 2 * TILE), F32)],
        ),
        out_shape=[jax.ShapeDtypeStruct((h, slots), BF16) for h in (TILE, first, TILE - first)],
        name="compact",
    )(start, place, amplitudes, pos)


def expand_kernel(tall, cuts, start, ids, *refs):
    n = len(cuts)
    n_in = 1 + max(c[0] for cut in cuts for c in cut)
    in_refs, pos_ref, out_refs, (held, sem) = refs[:n_in], refs[n_in], refs[n_in + 1 : -2], refs[-2:]
    slots = in_refs[0].shape[1]

    def copies():
        out = []
        for k, cut in enumerate(cuts):
            high = 0
            for which, low, size in cut:
                out.append(
                    pltpu.make_async_copy(
                        in_refs[which].at[pl.ds(low, size), :],
                        held.at[k, pl.ds(high, size), pl.ds(0, slots)],
                        sem.at[len(out)],
                    )
                )
                high += size
        return out

    @pl.when(pl.program_id(0) == 0)
    def _():
        for c in copies():
            c.start()
        for k in range(n):
            held[k, :, pl.ds(slots, TILE)] = jnp.zeros((TILE, TILE), BF16)
        for c in copies():
            c.wait()

    wide = pos_ref.shape[1]
    strip = pl.program_id(0) * (wide // TILE)
    for k in range(n):
        for i in range(tall):
            s = ids[k] * tall + i
            slot = pos_ref[pl.ds(s, 1), :]
            for b in range(wide // TILE):
                lanes = pl.ds(b * TILE, TILE)
                at = jnp.minimum(start[s, strip + b] // TILE * TILE, slots - TILE)
                at = pl.multiple_of(at, TILE)
                pick = (iota((2 * TILE, TILE), 0) + at == slot[:, b * TILE : (b + 1) * TILE]).astype(F32).astype(BF16)
                spread = jnp.dot(held[k, :, pl.ds(at, 2 * TILE)], pick, preferred_element_type=F32)
                out_refs[k][pl.ds(i * TILE, TILE), lanes] = spread.astype(BF16)


def expand(start, ids, pos, arrays, cuts, tall, wide=256):
    tiles, pairs = pos.shape
    slots = arrays[0].shape[1]
    n = len(cuts)
    flops = 2 * n * tall * pairs * TILE * 2 * TILE
    return pl.pallas_call(
        functools.partial(expand_kernel, tall, cuts),
        grid_spec=pltpu.PrefetchScalarGridSpec(
            num_scalar_prefetch=2,
            grid=(pairs // wide,),
            in_specs=whole(len(arrays), pltpu.HBM) + [pl.BlockSpec((tiles, wide), lambda i, *_: (0, i))],
            out_specs=[pl.BlockSpec((tall * TILE, wide), lambda i, *_: (0, i))] * n,
            scratch_shapes=[
                pltpu.VMEM((n, TILE, slots + TILE), BF16),
                pltpu.SemaphoreType.DMA((sum(len(c) for c in cuts),)),
            ],
        ),
        out_shape=[jax.ShapeDtypeStruct((tall * TILE, pairs), BF16)] * n,
        compiler_params=pltpu.CompilerParams(vmem_limit_bytes=VMEM_LIMIT),
        cost_estimate=pl.CostEstimate(flops=flops, bytes_accessed=n * tall * TILE * pairs * 3, transcendentals=0),
        name="expand",
    )(start, ids, *arrays, pos)


def product_kernel(n, first, which, *refs):
    a_refs, refs = refs[:5], refs[5:]
    b_refs, refs = refs[:n], refs[n:]
    if not first:
        sums, refs = refs[:2], refs[2:]
    outs, (a_all, b_all, sem) = refs[:-3], refs[-3:]
    rows = outs[0].shape[0]
    high, depth = a_all.shape[0], b_refs[0].shape[0]

    @pl.when(pl.program_id(0) == 0)
    def _():
        for k in range(n):
            target = a_all.at[:, pl.ds(k * depth, depth)]

            @pl.when(which[k] < 4)
            def _():
                pltpu.make_async_copy(a_refs[0].at[which[k]], target, sem.at[k]).start()

            for d in range(4):

                @pl.when(which[k] == 4 + d)
                def _():
                    pltpu.make_async_copy(a_refs[1 + d], target, sem.at[k]).start()

        for k in range(n):
            target = a_all.at[:, pl.ds(k * depth, depth)]
            pltpu.make_async_copy(a_refs[1], target, sem.at[k]).wait()

    for k in range(n):
        b_all[pl.ds(k * depth, depth), :] = b_refs[k][...]
    for h in range(2):
        total = jnp.dot(a_all[pl.ds(h * rows, rows), :], b_all[...], preferred_element_type=F32)
        outs[h][...] = total if first else sums[h][...] + total
    if first:
        flags = [a_all[pl.ds(2 * rows, FLAG_ROWS), pl.ds(k * depth, TILE)].astype(F32) for k in range(n)]
        outs[2][...] = functools.reduce(jnp.maximum, flags)


def product(which, a_parts, blocks, sums=None, wide=256):
    n, (depth, pairs) = len(blocks), blocks[0].shape
    high = a_parts[1].shape[0]
    rows = (high - FLAG_ROWS) // 2
    first = sums is None
    strip = lambda h: pl.BlockSpec((h, wide), lambda i, *_: (0, i))
    out = [jax.ShapeDtypeStruct((rows, pairs), F32)] * 2
    out_specs = [strip(rows)] * 2
    if first:
        out.append(jax.ShapeDtypeStruct((FLAG_ROWS, TILE), F32))
        out_specs.append(pl.BlockSpec((FLAG_ROWS, TILE), lambda i, *_: (0, 0)))
    return pl.pallas_call(
        functools.partial(product_kernel, n, first),
        grid_spec=pltpu.PrefetchScalarGridSpec(
            num_scalar_prefetch=1,
            grid=(pairs // wide,),
            in_specs=whole(5, pltpu.HBM) + [strip(depth)] * n + ([] if first else [strip(rows)] * 2),
            out_specs=out_specs,
            scratch_shapes=[
                pltpu.VMEM((high, n * depth), BF16),
                pltpu.VMEM((n * depth, wide), BF16),
                pltpu.SemaphoreType.DMA((n,)),
            ],
        ),
        out_shape=out,
        compiler_params=pltpu.CompilerParams(vmem_limit_bytes=VMEM_LIMIT),
        cost_estimate=pl.CostEstimate(
            flops=4 * rows * n * depth * pairs, bytes_accessed=2 * n * depth * (high + pairs) + 8 * rows * pairs, transcendentals=0
        ),
        name="product",
    )(which, *a_parts, *blocks, *(() if first else sums))


def shift(value, axis, by):
    n = lax.axis_size(axis)
    return lax.ppermute(value, axis, [(i, (i + by) % n) for i in range(n)])


def after(value, *others):
    return lax.optimization_barrier((value, *others))[0]


def dense(integrals, amplitudes, tile_pattern, pair_domain, tile_order):
    count = tile_order.shape[0]
    placed = (tile_order[:, None] == jnp.arange(count, dtype=I32)[None, :]).astype(F32)
    exact = functools.partial(jnp.dot, precision=lax.Precision.HIGHEST)
    pattern = exact(exact(placed, tile_pattern.astype(F32)), placed.T)
    domain = exact(placed, pair_domain.astype(F32))
    here = count // (lax.axis_size(ROW))
    pattern = lax.dynamic_slice_in_dim(pattern, lax.axis_index(ROW) * here, here, 0)
    mask = jnp.repeat(jnp.repeat(pattern, TILE, axis=0), TILE, axis=1).astype(BF16)
    screened = lax.all_gather(integrals, COL, axis=1, tiled=True) * mask
    domain = jnp.repeat(domain, TILE, axis=0).astype(BF16)
    restricted = lax.all_gather(amplitudes, ROW, axis=0, tiled=True) * domain
    return jnp.dot(screened, restricted, preferred_element_type=F32)


def on_device(integrals, amplitudes, tile_pattern, pair_domain, tile_order):
    zh, x, core = lax.axis_index("zh"), lax.axis_index("x"), lax.axis_index("core")
    zl, y = lax.axis_index("zl"), lax.axis_index("y")
    tall = amplitudes.shape[0] // TILE
    slots = amplitudes.shape[1] * tall * 5 // 9 // TILE * TILE
    first = TILE * 3 // 4
    place = jnp.stack([(zh * 4 + x) * 2 + core, zl * 4 + y, core]).astype(I32)
    keep, send, pos, start = plan(integrals, tile_pattern, pair_domain, tile_order, place, tall, slots)
    u, f, g = compact(start, place, amplitudes, pos, slots, first)

    a_here = jnp.concatenate([shift(send, "core", 1), keep], axis=0)
    a_own = lax.all_gather(a_here, "y", axis=0, tiled=False)
    there = shift(a_here, "zl", 1)

    up, um, pf = shift(u, "x", -1), shift(u, "x", 1), shift(f, "zh", 1)
    pg3 = shift(jnp.concatenate([g, up[first:], um[first:]], axis=0), "zh", 1)
    pf_up, pf_um = shift(pf, "x", -1), shift(pf, "x", 1)
    t_up, t_um = shift(there, "y", -1), shift(there, "y", 1)
    rest = TILE - first
    u2 = shift(um, "x", 1)
    pf2 = shift(pf_up, "x", -1)
    pg2 = shift(pg3[rest : 2 * rest], "x", -1)
    t_two = shift(t_um, "y", 1)
    a_parts = [a_own, there, t_up, t_two, t_um]

    def shard(dz, dx):
        return (((zh + dz) % 2) * 4 + (x + dx) % 4) * 2 + core

    def where(dz, dx):
        far, across = (zh + dz) % 2, (x + dx) % 4
        return jnp.where(far == zl, across, 4 + (across - y) % 4)

    def listed(of, pairs):
        return jnp.stack([of(*p) for p in pairs]).astype(I32)

    near, far, last = [(0, 0), (0, 1), (0, 3)], [(1, 0), (1, 1), (1, 3)], [(0, 2), (1, 2)]
    whole_cut = [[(k, 0, TILE)] for k in range(3)]
    blocks = expand(start, listed(shard, near), pos, [u, up, um], whole_cut, tall)
    far_cut = [[(k, 0, first), (3, k * rest, rest)] for k in range(3)]
    blocks += expand(start, listed(shard, far), pos, [pf, pf_up, pf_um, pg3], far_cut, tall)
    last_cut = [[(0, 0, TILE)], [(1, 0, first), (2, 0, rest)]]
    final = expand(start, listed(shard, last), pos, [u2, pf2, pg2], last_cut, tall)
    *sums, flags = product(listed(where, near + far), a_parts, blocks)
    other, own = product(listed(where, last), a_parts, final, sums)
    theirs = shift(other, "core", 1)
    return lax.cond(
        jnp.max(flags) > 0.5,
        lambda *args: dense(*args[:5]),
        lambda *args: args[5] + args[6],
        integrals,
        amplitudes,
        tile_pattern,
        pair_domain,
        tile_order,
        own,
        theirs,
    )


def solution(mesh):
    fine = Mesh(np.asarray(mesh.devices).reshape(SIZES), AXES)
    return jax.shard_map(
        on_device,
        mesh=fine,
        in_specs=(P(ROW, COL), P(ROW, COL), P(), P(None, COL), P()),
        out_specs=P(ROW, COL),
        check_vma=False,
    )
```

```python
import functools

import jax
import jax.numpy as jnp
import numpy as np
from jax import lax
from jax.experimental import pallas as pl
from jax.experimental.pallas import tpu as pltpu
from jax.sharding import Mesh, PartitionSpec as P

TILE = 128
AXES = ("zh", "x", "core", "zl", "y")
SIZES = (2, 4, 2, 2, 4)
ROW, COL = ("zh", "x", "core"), ("zl", "y")
BF16, F32, I32 = jnp.bfloat16, jnp.float32, jnp.int32
FLAG_ROWS = 8
VMEM_LIMIT = 60 << 20


def iota(shape, dim):
    return lax.broadcasted_iota(I32, shape, dim)


def whole(n, space=pltpu.VMEM):
    return [pl.BlockSpec(memory_space=space)] * n


def screen_kernel(tall, order, pattern, place, a_ref, keep_ref, send_ref):
    row, col, core = place[0], place[1], place[2]
    rows, cols = a_ref.shape
    half = cols // TILE // 2
    for i in range(rows // TILE):
        high = pl.ds(i * TILE, TILE)
        for j in range(half):
            for ref, base in ((keep_ref, core * half), (send_ref, (1 - core) * half)):
                tile = base + j
                on = pattern[order[row * tall + i], order[col * 2 * half + tile]]
                scale = on.astype(F32).astype(BF16)
                part = a_ref[high, pl.ds(pl.multiple_of(tile * TILE, TILE), TILE)]
                ref[high, pl.ds(j * TILE, TILE)] = part * scale


def screen(integrals, tile_pattern, tile_order, place, tall):
    rows, cols = integrals.shape
    return pl.pallas_call(
        functools.partial(screen_kernel, tall),
        grid_spec=pltpu.PrefetchScalarGridSpec(num_scalar_prefetch=3, grid=(), in_specs=whole(1), out_specs=whole(2)),
        out_shape=[jax.ShapeDtypeStruct((rows, cols // 2), BF16)] * 2,
        name="screen",
    )(tile_order, tile_pattern, place, integrals)


def plan_kernel(tall, slots, order, d_ref, pos_ref, start_ref, flag_ref, dom):
    tiles, pairs = dom.shape
    for s in range(tiles):
        dom[pl.ds(s, 1), :] = d_ref[pl.ds(order[s], 1), :]
    live = dom[...].astype(F32).astype(BF16)
    blocks = pairs // TILE
    spread = (iota((pairs, TILE), 0) // TILE == iota((pairs, TILE), 1)).astype(F32).astype(BF16)
    counts = jnp.dot(live, spread, preferred_element_type=F32)
    below = (iota((TILE, TILE), 0) < iota((TILE, TILE), 1)).astype(F32).astype(BF16)
    upto = (iota((TILE, TILE), 0) <= iota((TILE, TILE), 1)).astype(F32).astype(BF16)
    s0, s1 = iota((tiles, tiles), 0), iota((tiles, tiles), 1)
    before = ((s0 // tall == s1 // tall) & (s1 < s0)).astype(F32).astype(BF16)
    counted = counts.astype(BF16)
    ahead = jnp.sum(jnp.dot(before, counted, preferred_element_type=F32), axis=1, keepdims=True)
    starts = jnp.dot(counted, below, preferred_element_type=F32) + ahead
    start_ref[...] = starts.astype(I32)
    for b in range(blocks):
        lanes = pl.ds(b * TILE, TILE)
        here = live[:, b * TILE : (b + 1) * TILE]
        slot = jnp.dot(here, upto, preferred_element_type=F32) + (starts[:, b : b + 1] - 1.0)
        pos_ref[:, lanes] = jnp.where(dom[:, lanes] > 0, slot.astype(I32), -1)
    most = jnp.max(ahead + jnp.sum(counts, axis=1, keepdims=True), axis=0, keepdims=True)
    flag_ref[...] = jnp.broadcast_to(jnp.where(most > slots, 1.0, 0.0).astype(F32), flag_ref.shape).astype(BF16)


def plan(pair_domain, tile_order, tall, slots, cols):
    tiles, pairs = pair_domain.shape
    return pl.pallas_call(
        functools.partial(plan_kernel, tall, slots),
        grid_spec=pltpu.PrefetchScalarGridSpec(
            num_scalar_prefetch=1,
            grid=(),
            in_specs=whole(1),
            out_specs=whole(3),
            scratch_shapes=[pltpu.VMEM((tiles, pairs), I32)],
        ),
        out_shape=[
            jax.ShapeDtypeStruct((tiles, pairs), I32),
            jax.ShapeDtypeStruct((tiles, TILE), I32),
            jax.ShapeDtypeStruct((FLAG_ROWS, cols), BF16),
        ],
        name="plan",
    )(tile_order, pair_domain)


def compact_kernel(slots, start, place, b_ref, pos_ref, u_ref, total):
    tall = b_ref.shape[0] // TILE
    total[...] = jnp.zeros_like(total)
    for i in range(tall):
        s = place[0] * tall + i
        slot = pos_ref[pl.ds(s, 1), :]
        for b in range(b_ref.shape[1] // TILE):
            lanes = pl.ds(b * TILE, TILE)
            at = jnp.minimum(start[s, b] // TILE * TILE, slots)
            at = pl.multiple_of(at, TILE)
            pick = (iota((2 * TILE, TILE), 0) + at == slot[:, b * TILE : (b + 1) * TILE]).astype(F32).astype(BF16)
            moved = lax.dot_general(
                b_ref[pl.ds(i * TILE, TILE), lanes], pick, (((1,), (1,)), ((), ())), preferred_element_type=F32
            )
            total[:, pl.ds(at, 2 * TILE)] += moved
    u_ref[...] = total[:, :slots].astype(BF16)


def compact(start, place, amplitudes, pos, slots):
    return pl.pallas_call(
        functools.partial(compact_kernel, slots),
        grid_spec=pltpu.PrefetchScalarGridSpec(
            num_scalar_prefetch=2,
            grid=(),
            in_specs=whole(2),
            out_specs=pl.BlockSpec(memory_space=pltpu.VMEM),
            scratch_shapes=[pltpu.VMEM((TILE, slots + 2 * TILE), F32)],
        ),
        out_shape=jax.ShapeDtypeStruct((TILE, slots), BF16),
        name="compact",
    )(start, place, amplitudes, pos)


def product_kernel(tall, n, na, nb, first, start, ids, which, source, *refs):
    a_refs, in_refs, pos_ref, refs = refs[:na], refs[na : na + nb], refs[na + nb], refs[na + nb + 1 :]
    if not first:
        sums, refs = refs[:3], refs[3:]
    outs, (a_all, held, b_all, a_sem, sem) = refs[:3], refs[3:]
    rows = outs[0].shape[0]
    slots = in_refs[0].shape[1]
    depth = tall * TILE

    def fetch(options, choice, target, done):
        for j, option in enumerate(options):

            @pl.when(choice == j)
            def _(option=option):
                pltpu.make_async_copy(option, target, done).start()

    def a_slot(k):
        return a_all.at[:, pl.ds(k * depth, depth)]

    def b_slot(k):
        return held.at[k, :, pl.ds(0, slots)]

    @pl.when(pl.program_id(0) == 0)
    def _():
        for k in range(n):
            fetch(in_refs, source[k], b_slot(k), sem.at[k])
        for k in range(n):
            fetch(a_refs, which[k], a_slot(k), a_sem.at[k])
            held[k, :, pl.ds(slots, TILE)] = jnp.zeros((TILE, TILE), BF16)
        for k in range(n):
            pltpu.make_async_copy(in_refs[0], b_slot(k), sem.at[k]).wait()

    wide = pos_ref.shape[1]
    strip = pl.program_id(0) * (wide // TILE)
    lines = iota((2 * TILE, TILE), 0).astype(F32).astype(BF16)
    for k in range(n):
        for i in range(tall):
            s = ids[k] * tall + i
            slot = pos_ref[pl.ds(s, 1), :]
            for b in range(wide // TILE):
                at = jnp.minimum(start[s, strip + b] // TILE * TILE, slots - TILE)
                at = pl.multiple_of(at, TILE)
                here = slot[:, b * TILE : (b + 1) * TILE] - at
                here = jnp.where((here < 0) | (here >= 2 * TILE), -1, here).astype(F32).astype(BF16)
                pick = jnp.where(lines == here, jnp.ones((), BF16), jnp.zeros((), BF16))
                spread = jnp.dot(held[k, :, pl.ds(at, 2 * TILE)], pick, preferred_element_type=F32)
                b_all[pl.ds((k * tall + i) * TILE, TILE), pl.ds(b * TILE, TILE)] = spread.astype(BF16)

    @pl.when(pl.program_id(0) == 0)
    def _():
        for k in range(n):
            pltpu.make_async_copy(a_refs[0], a_slot(k), a_sem.at[k]).wait()

    for h in range(2):
        total = jnp.dot(a_all[pl.ds(h * rows, rows), :], b_all[...], preferred_element_type=F32)
        outs[h][...] = total if first else sums[h][...] + total
    flags = [a_all[pl.ds(2 * rows, FLAG_ROWS), pl.ds(k * depth, TILE)].astype(F32) for k in range(n)]
    if not first:
        flags.append(sums[2][...])
    outs[2][...] = functools.reduce(jnp.maximum, flags)


def product(start, ids, which, source, a_parts, arrays, pos, tall, sums=None, wide=512):
    n, (tiles, pairs) = ids.shape[0], pos.shape
    slots = arrays[0].shape[1]
    depth = tall * TILE
    high = a_parts[0].shape[0]
    rows = (high - FLAG_ROWS) // 2
    first = sums is None
    strip = lambda h: pl.BlockSpec((h, wide), lambda i, *_: (0, i))
    result = [strip(rows)] * 2 + [pl.BlockSpec((FLAG_ROWS, TILE), lambda i, *_: (0, 0))]
    return pl.pallas_call(
        functools.partial(product_kernel, tall, n, len(a_parts), len(arrays), first),
        grid_spec=pltpu.PrefetchScalarGridSpec(
            num_scalar_prefetch=4,
            grid=(pairs // wide,),
            in_specs=whole(len(a_parts) + len(arrays), pltpu.HBM) + [strip(tiles)] + ([] if first else result),
            out_specs=result,
            scratch_shapes=[
                pltpu.VMEM((high, n * depth), BF16),
                pltpu.VMEM((n, TILE, slots + TILE), BF16),
                pltpu.VMEM((n * depth, wide), BF16),
                pltpu.SemaphoreType.DMA((n,)),
                pltpu.SemaphoreType.DMA((n,)),
            ],
        ),
        out_shape=[jax.ShapeDtypeStruct((rows, pairs), F32)] * 2 + [jax.ShapeDtypeStruct((FLAG_ROWS, TILE), F32)],
        compiler_params=pltpu.CompilerParams(vmem_limit_bytes=VMEM_LIMIT),
        cost_estimate=pl.CostEstimate(
            flops=4 * rows * n * depth * pairs, bytes_accessed=2 * n * depth * (high + pairs) + 8 * rows * pairs, transcendentals=0
        ),
        name="product",
    )(start, ids, which, source, *a_parts, *arrays, pos, *(() if first else sums))


def shift(value, axis, by):
    n = lax.axis_size(axis)
    return lax.ppermute(value, axis, [(i, (i + by) % n) for i in range(n)])


def together(*values):
    return lax.optimization_barrier(values)


def dense(integrals, amplitudes, tile_pattern, pair_domain, tile_order):
    count = tile_order.shape[0]
    placed = (tile_order[:, None] == jnp.arange(count, dtype=I32)[None, :]).astype(F32)
    exact = functools.partial(jnp.dot, precision=lax.Precision.HIGHEST)
    pattern = exact(exact(placed, tile_pattern.astype(F32)), placed.T)
    domain = exact(placed, pair_domain.astype(F32))
    here = count // (lax.axis_size(ROW))
    pattern = lax.dynamic_slice_in_dim(pattern, lax.axis_index(ROW) * here, here, 0)
    mask = jnp.repeat(jnp.repeat(pattern, TILE, axis=0), TILE, axis=1).astype(BF16)
    screened = lax.all_gather(integrals, COL, axis=1, tiled=True) * mask
    domain = jnp.repeat(domain, TILE, axis=0).astype(BF16)
    restricted = lax.all_gather(amplitudes, ROW, axis=0, tiled=True) * domain
    return jnp.dot(screened, restricted, preferred_element_type=F32)


def on_device(integrals, amplitudes, tile_pattern, pair_domain, tile_order):
    zh, x, core = lax.axis_index("zh"), lax.axis_index("x"), lax.axis_index("core")
    zl, y = lax.axis_index("zl"), lax.axis_index("y")
    tall = amplitudes.shape[0] // TILE
    slots = amplitudes.shape[1] * tall * 5 // 9 // TILE * TILE
    place = jnp.stack([(zh * 4 + x) * 2 + core, zl * 4 + y, core]).astype(I32)
    keep, send = screen(integrals, tile_pattern, tile_order, place, tall)
    recv = shift(send, "core", 1)
    pos, start, flags = plan(pair_domain, tile_order, tall, slots, keep.shape[1])
    u = compact(start, place, amplitudes, pos, slots)
    recv, u = together(recv, u)
    mine = jnp.concatenate([recv, keep, flags], axis=0)

    up, um = shift(u, "x", -1), shift(u, "x", 1)
    ap, am, there = shift(mine, "y", -1), shift(mine, "y", 1), shift(mine, "zl", 1)
    up, um, ap, am, there = together(up, um, ap, am, there)
    u2, q = shift(um, "x", 1), shift(u, "zh", 1)
    tp, tm = shift(there, "y", -1), shift(there, "y", 1)
    u2, q, tp, tm = together(u2, q, tp, tm)
    qp, qm, q2 = shift(q, "x", -1), shift(q, "x", 1), shift(u2, "zh", 1)
    a2, t2 = shift(am, "y", 1), shift(tp, "y", -1)

    same = (zh == zl).astype(I32)

    def blocks(picks, n_hops):
        ids, which, source = [], [], []
        for dz, hop in picks:
            across = (y + hop) % 4
            ids.append((((zh + dz) % 2) * 4 + across) * 2 + core)
            own = same if dz == 0 else 1 - same
            which.append(n_hops.index(hop) + (1 - own) * len(n_hops))
            source.append(dz * 4 + (across - x) % 4)
        return [jnp.stack(v).astype(I32) for v in (ids, which, source)]

    near, far = [u, up, u2, um], [q, qp, q2, qm]
    sums = product(start, *blocks([(0, 0), (0, 1), (0, 3)], [0, 1, 3]), [mine, ap, am, there, tp, tm], near, pos, tall)
    other, own, flags = product(
        start,
        *blocks([(0, 2), (1, 0), (1, 1), (1, 2), (1, 3)], [0, 1, 2, 3]),
        [mine, ap, a2, am, there, tp, t2, tm],
        near + far,
        pos,
        tall,
        sums,
    )
    theirs = shift(other, "core", 1)
    return lax.cond(
        jnp.max(flags) > 0.5,
        lambda *args: dense(*args[:5]),
        lambda *args: args[5] + args[6],
        integrals,
        amplitudes,
        tile_pattern,
        pair_domain,
        tile_order,
        own,
        theirs,
    )


def solution(mesh):
    fine = Mesh(np.asarray(mesh.devices).reshape(SIZES), AXES)
    return jax.shard_map(
        on_device,
        mesh=fine,
        in_specs=(P(ROW, COL), P(ROW, COL), P(), P(None, COL), P()),
        out_specs=P(ROW, COL),
        check_vma=False,
    )
```

```python
import functools

import jax
import jax.numpy as jnp
import numpy as np
from jax import lax
from jax.experimental import pallas as pl
from jax.experimental.pallas import tpu as pltpu
from jax.sharding import Mesh, PartitionSpec as P

TILE = 128
AXES = ("zh", "x", "core", "zl", "y")
SIZES = (2, 4, 2, 2, 4)
ROW, COL = ("zh", "x", "core"), ("zl", "y")
BF16, F32, I32 = jnp.bfloat16, jnp.float32, jnp.int32
FLAG_ROWS = 8
VMEM_LIMIT = 60 << 20


def where_am_i():
    row = (lax.axis_index("zh") * 4 + lax.axis_index("x")) * 2 + lax.axis_index("core")
    return row, lax.axis_index("zl") * 4 + lax.axis_index("y"), lax.axis_index("core")


def iota(shape, dim):
    return lax.broadcasted_iota(I32, shape, dim)


def whole(n, space=pltpu.VMEM):
    return [pl.BlockSpec(memory_space=space)] * n


def join_kernel(tall, order, pattern, over_ref, a_ref, recv_ref, join_ref):
    row, col, core = where_am_i()
    rows, cols = a_ref.shape
    half = cols // TILE // 2
    for which, ref in ((1, recv_ref), (0, a_ref)):
        block = jnp.bitwise_xor(row, which)
        for i in range(rows // TILE):
            high = pl.ds(i * TILE, TILE)
            for j in range(half):
                tile = core * half + j
                on = pattern[order[block * tall + i], order[col * 2 * half + tile]]
                scale = on.astype(F32).astype(BF16)
                part = ref[high, pl.ds(pl.multiple_of(tile * TILE, TILE), TILE)]
                join_ref[pl.ds((1 - which) * rows + i * TILE, TILE), pl.ds(j * TILE, TILE)] = part * scale
    join_ref[pl.ds(2 * rows, FLAG_ROWS), :] = over_ref[...]


def join(integrals, recv, over, tile_pattern, tile_order, tall):
    rows, cols = integrals.shape
    return pl.pallas_call(
        functools.partial(join_kernel, tall),
        grid_spec=pltpu.PrefetchScalarGridSpec(
            num_scalar_prefetch=2, grid=(), in_specs=whole(3), out_specs=pl.BlockSpec(memory_space=pltpu.VMEM)
        ),
        out_shape=jax.ShapeDtypeStruct((2 * rows + FLAG_ROWS, cols // 2), BF16),
        name="join",
    )(tile_order, tile_pattern, over, integrals, recv)


def pack_kernel(
    tall, slots, order, d_ref, b_ref, pos_ref, start_ref, u_ref, over_ref, dom, total, start, sem
):
    tiles, pairs = dom.shape
    for s in range(tiles):
        dom[pl.ds(s, 1), :] = d_ref[pl.ds(order[s], 1), :]
    live = dom[...].astype(F32).astype(BF16)
    blocks = pairs // TILE
    spread = (iota((pairs, TILE), 0) // TILE == iota((pairs, TILE), 1)).astype(F32).astype(BF16)
    counts = jnp.dot(live, spread, preferred_element_type=F32)
    below = (iota((TILE, TILE), 0) < iota((TILE, TILE), 1)).astype(F32).astype(BF16)
    upto = (iota((TILE, TILE), 0) <= iota((TILE, TILE), 1)).astype(F32).astype(BF16)
    s0, s1 = iota((tiles, tiles), 0), iota((tiles, tiles), 1)
    before = ((s0 // tall == s1 // tall) & (s1 < s0)).astype(F32).astype(BF16)
    counted = counts.astype(BF16)
    ahead = jnp.sum(jnp.dot(before, counted, preferred_element_type=F32), axis=1, keepdims=True)
    starts = jnp.dot(counted, below, preferred_element_type=F32) + ahead
    start_ref[...] = starts.astype(I32)
    copy = pltpu.make_async_copy(start_ref, start, sem)
    copy.start()
    for b in range(blocks):
        lanes = pl.ds(b * TILE, TILE)
        here = live[:, b * TILE : (b + 1) * TILE]
        slot = jnp.dot(here, upto, preferred_element_type=F32) + (starts[:, b : b + 1] - 1.0)
        pos_ref[:, lanes] = jnp.where(dom[:, lanes] > 0, slot.astype(I32), -1)
    most = jnp.max(ahead + jnp.sum(counts, axis=1, keepdims=True), axis=0, keepdims=True)
    flag = jnp.where(most > slots, 1.0, 0.0).astype(F32)
    over_ref[...] = jnp.broadcast_to(flag, over_ref.shape).astype(BF16)
    total[...] = jnp.zeros_like(total)
    copy.wait()
    for i in range(tall):
        s = where_am_i()[0] * tall + i
        slot = pos_ref[pl.ds(s, 1), :]
        for b in range(blocks):
            lanes = pl.ds(b * TILE, TILE)
            at = jnp.minimum(start[s, b] // TILE * TILE, slots)
            at = pl.multiple_of(at, TILE)
            pick = (iota((2 * TILE, TILE), 0) + at == slot[:, b * TILE : (b + 1) * TILE]).astype(F32).astype(BF16)
            moved = lax.dot_general(
                b_ref[pl.ds(i * TILE, TILE), lanes], pick, (((1,), (1,)), ((), ())), preferred_element_type=F32
            )
            total[:, pl.ds(at, 2 * TILE)] += moved
    u_ref[...] = total[:, :slots].astype(BF16)


def pack(pair_domain, amplitudes, tile_order, tall, slots, cols):
    tiles, pairs = pair_domain.shape
    return pl.pallas_call(
        functools.partial(pack_kernel, tall, slots),
        grid_spec=pltpu.PrefetchScalarGridSpec(
            num_scalar_prefetch=1,
            grid=(),
            in_specs=whole(2),
            out_specs=whole(4),
            scratch_shapes=[
                pltpu.VMEM((tiles, pairs), I32),
                pltpu.VMEM((TILE, slots + 2 * TILE), F32),
                pltpu.SMEM((tiles, TILE), I32),
                pltpu.SemaphoreType.DMA(()),
            ],
        ),
        out_shape=[
            jax.ShapeDtypeStruct((tiles, pairs), I32),
            jax.ShapeDtypeStruct((tiles, TILE), I32),
            jax.ShapeDtypeStruct((TILE, slots), BF16),
            jax.ShapeDtypeStruct((FLAG_ROWS, cols), BF16),
        ],
        name="pack",
    )(tile_order, pair_domain, amplitudes)


def product_kernel(tall, picks, hops, first, wide, start_ref, *refs):
    n, nh = len(picks), len(hops)
    a_refs, refs = refs[: 2 * nh], refs[2 * nh :]
    in_refs, pos_ref, refs = refs[:8], refs[8], refs[9:]
    if not first:
        sums, flags_ref, refs = refs[:2], refs[2], refs[3:]
    outs, flag_out, (a_all, held, b_all, held_sums, start, a_sem, sem, in_sem, out_sem, start_sem) = refs[:2], refs[2], refs[3:]
    rows, pairs = outs[0].shape
    slots = in_refs[0].shape[1]
    depth = tall * TILE
    zh, x, core, zl, y = (lax.axis_index(axis) for axis in AXES)
    starts = pltpu.make_async_copy(start_ref, start, start_sem)
    starts.start()

    def a_slot(k):
        return a_all.at[:, pl.ds(k * depth, depth)]

    def b_slot(k):
        return held.at[k, :, pl.ds(0, slots)]

    ids = []
    for k, (dz, hop) in enumerate(picks):
        across, far = (y + hop) % 4, zh if dz == 0 else 1 - zh
        ids.append((far * 4 + across) * 2 + core)
        for dx in range(4):

            @pl.when((across - x + 4) % 4 == dx)
            def _(k=k, option=in_refs[4 * dz + dx]):
                pltpu.make_async_copy(option, b_slot(k), sem.at[k]).start()

        for own in range(2):

            @pl.when((far == zl) == (own == 0))
            def _(k=k, option=a_refs[own * nh + hops.index(hop)]):
                pltpu.make_async_copy(option, a_slot(k), a_sem.at[k]).start()

    strips = pairs // wide

    def strip(b):
        return pl.ds(b * wide, wide)

    if not first:
        loads = [
            [pltpu.make_async_copy(sums[h].at[:, strip(b)], held_sums.at[h, :, strip(b)], in_sem.at[h, b]) for h in range(2)]
            for b in range(strips)
        ]
        for pair in loads:
            for load in pair:
                load.start()
    for k in range(n):
        held[k, :, pl.ds(slots, TILE)] = jnp.zeros((TILE, TILE), BF16)

    lines = iota((2 * TILE, TILE), 0).astype(F32).astype(BF16)
    stores = []
    starts.wait()
    for b in range(strips):
        for k in range(n):
            if b == 0:
                pltpu.make_async_copy(in_refs[0], b_slot(k), sem.at[k]).wait()
            for i in range(tall):
                s = ids[k] * tall + i
                slot = pos_ref[pl.ds(s, 1), :]
                for c in range(wide // TILE):
                    block = b * (wide // TILE) + c
                    at = jnp.minimum(start[s, block] // TILE * TILE, slots - TILE)
                    at = pl.multiple_of(at, TILE)
                    here = slot[:, block * TILE : (block + 1) * TILE] - at
                    here = jnp.where((here < 0) | (here >= 2 * TILE), -1, here).astype(F32).astype(BF16)
                    pick = jnp.where(lines == here, jnp.ones((), BF16), jnp.zeros((), BF16))
                    spread = jnp.dot(held[k, :, pl.ds(at, 2 * TILE)], pick, preferred_element_type=F32)
                    b_all[pl.ds((k * tall + i) * TILE, TILE), pl.ds(c * TILE, TILE)] = spread.astype(BF16)
        if b == 0:
            for k in range(n):
                pltpu.make_async_copy(a_refs[0], a_slot(k), a_sem.at[k]).wait()
        for h in range(2):
            total = jnp.dot(a_all[pl.ds(h * rows, rows), :], b_all[...], preferred_element_type=F32)
            if not first:
                loads[b][h].wait()
                total += held_sums[h, :, strip(b)]
            held_sums[h, :, strip(b)] = total
            store = pltpu.make_async_copy(held_sums.at[h, :, strip(b)], outs[h].at[:, strip(b)], out_sem.at[h, b])
            store.start()
            stores.append(store)
    flags = [a_all[pl.ds(2 * rows, FLAG_ROWS), pl.ds(k * depth, TILE)].astype(F32) for k in range(n)]
    if not first:
        flags.append(flags_ref[...])
    flag_out[...] = functools.reduce(jnp.maximum, flags)
    for store in stores:
        store.wait()


def product(start, picks, hops, a_parts, arrays, pos, tall, sums=None, wide=1536):
    n, (tiles, pairs) = len(picks), pos.shape
    slots = arrays[0].shape[1]
    depth = tall * TILE
    high = a_parts[0].shape[0]
    rows = (high - FLAG_ROWS) // 2
    first = sums is None
    strips = pairs // wide
    hbm = pl.BlockSpec(memory_space=pltpu.HBM)
    vmem = pl.BlockSpec(memory_space=pltpu.VMEM)
    return pl.pallas_call(
        functools.partial(product_kernel, tall, picks, hops, first, wide),
        grid_spec=pltpu.PrefetchScalarGridSpec(
            num_scalar_prefetch=0,
            grid=(),
            in_specs=[hbm] * (len(a_parts) + 9) + [vmem] + ([] if first else [hbm, hbm, vmem]),
            out_specs=[hbm, hbm, vmem],
            scratch_shapes=[
                pltpu.VMEM((high, n * depth), BF16),
                pltpu.VMEM((n, TILE, slots + TILE), BF16),
                pltpu.VMEM((n * depth, wide), BF16),
                pltpu.VMEM((2, rows, pairs), F32),
                pltpu.SMEM((tiles, TILE), I32),
                pltpu.SemaphoreType.DMA((n,)),
                pltpu.SemaphoreType.DMA((n,)),
                pltpu.SemaphoreType.DMA((2, strips)),
                pltpu.SemaphoreType.DMA((2, strips)),
                pltpu.SemaphoreType.DMA(()),
            ],
        ),
        out_shape=[jax.ShapeDtypeStruct((rows, pairs), F32)] * 2 + [jax.ShapeDtypeStruct((FLAG_ROWS, TILE), F32)],
        compiler_params=pltpu.CompilerParams(vmem_limit_bytes=VMEM_LIMIT),
        cost_estimate=pl.CostEstimate(
            flops=4 * rows * n * depth * pairs, bytes_accessed=2 * n * depth * (high + pairs) + 8 * rows * pairs, transcendentals=0
        ),
        name="product",
    )(start, *a_parts, *arrays, pos, *(() if first else sums))


def shift(value, axis, by):
    n = lax.axis_size(axis)
    return lax.ppermute(value, axis, [(i, (i + by) % n) for i in range(n)])


def together(*values):
    return lax.optimization_barrier(values)


def dense(integrals, amplitudes, tile_pattern, pair_domain, tile_order):
    count = tile_order.shape[0]
    placed = (tile_order[:, None] == jnp.arange(count, dtype=I32)[None, :]).astype(F32)
    exact = functools.partial(jnp.dot, precision=lax.Precision.HIGHEST)
    pattern = exact(exact(placed, tile_pattern.astype(F32)), placed.T)
    domain = exact(placed, pair_domain.astype(F32))
    here = count // (lax.axis_size(ROW))
    pattern = lax.dynamic_slice_in_dim(pattern, lax.axis_index(ROW) * here, here, 0)
    mask = jnp.repeat(jnp.repeat(pattern, TILE, axis=0), TILE, axis=1).astype(BF16)
    screened = lax.all_gather(integrals, COL, axis=1, tiled=True) * mask
    domain = jnp.repeat(domain, TILE, axis=0).astype(BF16)
    restricted = lax.all_gather(amplitudes, ROW, axis=0, tiled=True) * domain
    return jnp.dot(screened, restricted, preferred_element_type=F32)


def on_device(integrals, amplitudes, tile_pattern, pair_domain, tile_order):
    tall = amplitudes.shape[0] // TILE
    slots = amplitudes.shape[1] * tall * 5 // 9 // TILE * TILE
    recv = shift(integrals, "core", 1)
    pos, start, u, over = pack(pair_domain, amplitudes, tile_order, tall, slots, integrals.shape[1] // 2)
    mine = join(integrals, recv, over, tile_pattern, tile_order, tall)

    up, um = shift(u, "x", -1), shift(u, "x", 1)
    ap, am, there = shift(mine, "y", -1), shift(mine, "y", 1), shift(mine, "zl", 1)
    up, um, ap, am, there = together(up, um, ap, am, there)
    u2, q = shift(um, "x", 1), shift(u, "zh", 1)
    tp, tm = shift(there, "y", -1), shift(there, "y", 1)
    u2, q, tp, tm = together(u2, q, tp, tm)
    qp, qm, q2 = shift(q, "x", -1), shift(q, "x", 1), shift(u2, "zh", 1)
    a2, t2 = shift(am, "y", 1), shift(tp, "y", -1)

    arrays = [u, up, u2, um]
    early, late = ((0, 0), (0, 1), (0, 3)), ((0, 2), (1, 0), (1, 1), (1, 2), (1, 3))
    sums = product(start, early, (0, 1, 3), [mine, ap, am, there, tp, tm], arrays * 2, pos, tall)
    arrays += [q, qp, q2, qm]
    a_parts = [mine, ap, a2, am, there, tp, t2, tm]
    other, own, flags = product(start, late, (0, 1, 2, 3), a_parts, arrays, pos, tall, sums)
    theirs = shift(other, "core", 1)
    return lax.cond(
        jnp.max(flags) > 0.5,
        lambda *args: dense(*args[:5]),
        lambda *args: args[5] + args[6],
        integrals,
        amplitudes,
        tile_pattern,
        pair_domain,
        tile_order,
        own,
        theirs,
    )


def solution(mesh):
    fine = Mesh(np.asarray(mesh.devices).reshape(SIZES), AXES)
    return jax.shard_map(
        on_device,
        mesh=fine,
        in_specs=(P(ROW, COL), P(ROW, COL), P(), P(None, COL), P()),
        out_specs=P(ROW, COL),
        check_vma=False,
    )
```

```python
import functools

import jax
import jax.numpy as jnp
import numpy as np
from jax import lax
from jax.experimental import pallas as pl
from jax.experimental.pallas import tpu as pltpu
from jax.sharding import Mesh, PartitionSpec as P

TILE = 128
AXES = ("zh", "x", "core", "zl", "y")
SIZES = (2, 4, 2, 2, 4)
ROW, COL = ("zh", "x", "core"), ("zl", "y")
BF16, F32, I32 = jnp.bfloat16, jnp.float32, jnp.int32
FLAG_ROWS = 8
VMEM_LIMIT, LAST_LIMIT = 255 << 18, 60 << 20


def where_am_i():
    row = (lax.axis_index("zh") * 4 + lax.axis_index("x")) * 2 + lax.axis_index("core")
    return row, lax.axis_index("zl") * 4 + lax.axis_index("y"), lax.axis_index("core")


def iota(shape, dim):
    return lax.broadcasted_iota(I32, shape, dim)


def whole(n, space=pltpu.VMEM):
    return [pl.BlockSpec(memory_space=space)] * n


def join_kernel(tall, order, pattern, over_ref, a_ref, recv_ref, join_ref):
    row, col, core = where_am_i()
    rows, cols = a_ref.shape
    half = cols // TILE // 2
    for which, ref in ((1, recv_ref), (0, a_ref)):
        block = jnp.bitwise_xor(row, which)
        for i in range(rows // TILE):
            high = pl.ds(i * TILE, TILE)
            for j in range(half):
                tile = core * half + j
                on = pattern[order[block * tall + i], order[col * 2 * half + tile]]
                scale = on.astype(F32).astype(BF16)
                part = ref[high, pl.ds(pl.multiple_of(tile * TILE, TILE), TILE)]
                join_ref[pl.ds((1 - which) * rows + i * TILE, TILE), pl.ds(j * TILE, TILE)] = part * scale
    join_ref[pl.ds(2 * rows, FLAG_ROWS), :] = over_ref[...]


def join(integrals, recv, over, tile_pattern, tile_order, tall):
    rows, cols = integrals.shape
    return pl.pallas_call(
        functools.partial(join_kernel, tall),
        grid_spec=pltpu.PrefetchScalarGridSpec(
            num_scalar_prefetch=2, grid=(), in_specs=whole(3), out_specs=pl.BlockSpec(memory_space=pltpu.VMEM)
        ),
        out_shape=jax.ShapeDtypeStruct((2 * rows + FLAG_ROWS, cols // 2), BF16),
        compiler_params=pltpu.CompilerParams(vmem_limit_bytes=VMEM_LIMIT),
        name="join",
    )(tile_order, tile_pattern, over, integrals, recv)


def pack_kernel(
    tall, slots, order, d_ref, b_ref, pos_ref, start_ref, u_ref, over_ref, dom, total, start, sem
):
    tiles, pairs = dom.shape
    for s in range(tiles):
        dom[pl.ds(s, 1), :] = d_ref[pl.ds(order[s], 1), :]
    live = dom[...].astype(F32).astype(BF16)
    blocks = pairs // TILE
    spread = (iota((pairs, TILE), 0) // TILE == iota((pairs, TILE), 1)).astype(F32).astype(BF16)
    counts = jnp.dot(live, spread, preferred_element_type=F32)
    below = (iota((TILE, TILE), 0) < iota((TILE, TILE), 1)).astype(F32).astype(BF16)
    upto = (iota((TILE, TILE), 0) <= iota((TILE, TILE), 1)).astype(F32).astype(BF16)
    s0, s1 = iota((tiles, tiles), 0), iota((tiles, tiles), 1)
    before = ((s0 // tall == s1 // tall) & (s1 < s0)).astype(F32).astype(BF16)
    counted = counts.astype(BF16)
    ahead = jnp.sum(jnp.dot(before, counted, preferred_element_type=F32), axis=1, keepdims=True)
    starts = jnp.dot(counted, below, preferred_element_type=F32) + ahead
    start_ref[...] = starts.astype(I32)
    copy = pltpu.make_async_copy(start_ref, start, sem)
    copy.start()
    for b in range(blocks):
        lanes = pl.ds(b * TILE, TILE)
        here = live[:, b * TILE : (b + 1) * TILE]
        slot = jnp.dot(here, upto, preferred_element_type=F32) + (starts[:, b : b + 1] - 1.0)
        pos_ref[:, lanes] = jnp.where(dom[:, lanes] > 0, slot.astype(I32), -1)
    most = jnp.max(ahead + jnp.sum(counts, axis=1, keepdims=True), axis=0, keepdims=True)
    flag = jnp.where(most > slots, 1.0, 0.0).astype(F32)
    over_ref[...] = jnp.broadcast_to(flag, over_ref.shape).astype(BF16)
    total[...] = jnp.zeros_like(total)
    copy.wait()
    for i in range(tall):
        s = where_am_i()[0] * tall + i
        slot = pos_ref[pl.ds(s, 1), :]
        for b in range(blocks):
            lanes = pl.ds(b * TILE, TILE)
            at = jnp.minimum(start[s, b] // TILE * TILE, slots)
            at = pl.multiple_of(at, TILE)
            pick = (iota((2 * TILE, TILE), 0) + at == slot[:, b * TILE : (b + 1) * TILE]).astype(F32).astype(BF16)
            moved = lax.dot_general(
                b_ref[pl.ds(i * TILE, TILE), lanes], pick, (((1,), (1,)), ((), ())), preferred_element_type=F32
            )
            total[:, pl.ds(at, 2 * TILE)] += moved
    u_ref[...] = total[:, :slots].astype(BF16)


def pack(pair_domain, amplitudes, tile_order, tall, slots, cols):
    tiles, pairs = pair_domain.shape
    return pl.pallas_call(
        functools.partial(pack_kernel, tall, slots),
        grid_spec=pltpu.PrefetchScalarGridSpec(
            num_scalar_prefetch=1,
            grid=(),
            in_specs=whole(2),
            out_specs=whole(4),
            scratch_shapes=[
                pltpu.VMEM((tiles, pairs), I32),
                pltpu.VMEM((TILE, slots + 2 * TILE), F32),
                pltpu.SMEM((tiles, TILE), I32),
                pltpu.SemaphoreType.DMA(()),
            ],
        ),
        out_shape=[
            jax.ShapeDtypeStruct((tiles, pairs), I32),
            jax.ShapeDtypeStruct((tiles, TILE), I32),
            jax.ShapeDtypeStruct((TILE, slots), BF16),
            jax.ShapeDtypeStruct((FLAG_ROWS, cols), BF16),
        ],
        compiler_params=pltpu.CompilerParams(vmem_limit_bytes=VMEM_LIMIT),
        name="pack",
    )(tile_order, pair_domain, amplitudes)


def product_kernel(tall, picks, hops, first, wide, start_ref, *refs):
    n, nh = len(picks), len(hops)
    a_refs, refs = refs[: 2 * nh], refs[2 * nh :]
    in_refs, pos_ref, refs = refs[:8], refs[8], refs[9:]
    if not first:
        sums, flags_ref, refs = refs[:2], refs[2], refs[3:]
    outs, flag_out, (a_all, held, b_all, held_sums, start, a_sem, sem, in_sem, out_sem, start_sem) = refs[:2], refs[2], refs[3:]
    rows, pairs = outs[0].shape
    slots = in_refs[0].shape[1]
    depth = tall * TILE
    zh, x, core, zl, y = (lax.axis_index(axis) for axis in AXES)
    starts = pltpu.make_async_copy(start_ref, start, start_sem)
    starts.start()

    def a_slot(k):
        return a_all.at[:, pl.ds(k * depth, depth)]

    def b_slot(k):
        return held.at[k, :, pl.ds(0, slots)]

    ids = []
    for k, (dz, hop) in enumerate(picks):
        across, far = (y + hop) % 4, zh if dz == 0 else 1 - zh
        ids.append((far * 4 + across) * 2 + core)
        for dx in range(4):

            @pl.when((across - x + 4) % 4 == dx)
            def _(k=k, option=in_refs[4 * dz + dx]):
                pltpu.make_async_copy(option, b_slot(k), sem.at[k]).start()

        for own in range(2):

            @pl.when((far == zl) == (own == 0))
            def _(k=k, option=a_refs[own * nh + hops.index(hop)]):
                pltpu.make_async_copy(option, a_slot(k), a_sem.at[k]).start()

    strips = pairs // wide

    def strip(b):
        return pl.ds(b * wide, wide)

    if not first:
        loads = [
            [pltpu.make_async_copy(sums[h].at[:, strip(b)], held_sums.at[h, :, strip(b)], in_sem.at[h, b]) for h in range(2)]
            for b in range(strips)
        ]
        for pair in loads:
            for load in pair:
                load.start()
    for k in range(n):
        held[k, :, pl.ds(slots, TILE)] = jnp.zeros((TILE, TILE), BF16)

    lines = iota((2 * TILE, TILE), 0).astype(F32).astype(BF16)
    stores = []
    starts.wait()
    for b in range(strips):
        for k in range(n):
            if b == 0:
                pltpu.make_async_copy(in_refs[0], b_slot(k), sem.at[k]).wait()
            for i in range(tall):
                s = ids[k] * tall + i
                slot = pos_ref[pl.ds(s, 1), :]
                for c in range(wide // TILE):
                    block = b * (wide // TILE) + c
                    at = jnp.minimum(start[s, block] // TILE * TILE, slots - TILE)
                    at = pl.multiple_of(at, TILE)
                    here = slot[:, block * TILE : (block + 1) * TILE] - at
                    here = jnp.where((here < 0) | (here >= 2 * TILE), -1, here).astype(F32).astype(BF16)
                    pick = jnp.where(lines == here, jnp.ones((), BF16), jnp.zeros((), BF16))
                    spread = jnp.dot(held[k, :, pl.ds(at, 2 * TILE)], pick, preferred_element_type=F32)
                    b_all[pl.ds((k * tall + i) * TILE, TILE), pl.ds(c * TILE, TILE)] = spread.astype(BF16)
        if b == 0:
            for k in range(n):
                pltpu.make_async_copy(a_refs[0], a_slot(k), a_sem.at[k]).wait()
        for h in range(2):
            total = jnp.dot(a_all[pl.ds(h * rows, rows), :], b_all[...], preferred_element_type=F32)
            if not first:
                loads[b][h].wait()
                total += held_sums[h, :, strip(b)]
            held_sums[h, :, strip(b)] = total
            store = pltpu.make_async_copy(held_sums.at[h, :, strip(b)], outs[h].at[:, strip(b)], out_sem.at[h, b])
            store.start()
            stores.append(store)
    flags = [a_all[pl.ds(2 * rows, FLAG_ROWS), pl.ds(k * depth, TILE)].astype(F32) for k in range(n)]
    if not first:
        flags.append(flags_ref[...])
    flag_out[...] = functools.reduce(jnp.maximum, flags)
    for store in stores:
        store.wait()


def product(start, picks, hops, a_parts, arrays, pos, tall, sums=None, wide=1536):
    n, (tiles, pairs) = len(picks), pos.shape
    slots = arrays[0].shape[1]
    depth = tall * TILE
    high = a_parts[0].shape[0]
    rows = (high - FLAG_ROWS) // 2
    first = sums is None
    strips = pairs // wide
    hbm = pl.BlockSpec(memory_space=pltpu.HBM)
    vmem = pl.BlockSpec(memory_space=pltpu.VMEM)
    return pl.pallas_call(
        functools.partial(product_kernel, tall, picks, hops, first, wide),
        grid_spec=pltpu.PrefetchScalarGridSpec(
            num_scalar_prefetch=0,
            grid=(),
            in_specs=[hbm] * (len(a_parts) + 9) + [vmem] + ([] if first else [hbm, hbm, vmem]),
            out_specs=[hbm, hbm, vmem],
            scratch_shapes=[
                pltpu.VMEM((high, n * depth), BF16),
                pltpu.VMEM((n, TILE, slots + TILE), BF16),
                pltpu.VMEM((n * depth, wide), BF16),
                pltpu.VMEM((2, rows, pairs), F32),
                pltpu.SMEM((tiles, TILE), I32),
                pltpu.SemaphoreType.DMA((n,)),
                pltpu.SemaphoreType.DMA((n,)),
                pltpu.SemaphoreType.DMA((2, strips)),
                pltpu.SemaphoreType.DMA((2, strips)),
                pltpu.SemaphoreType.DMA(()),
            ],
        ),
        out_shape=[jax.ShapeDtypeStruct((rows, pairs), F32)] * 2 + [jax.ShapeDtypeStruct((FLAG_ROWS, TILE), F32)],
        compiler_params=pltpu.CompilerParams(vmem_limit_bytes=VMEM_LIMIT if first else LAST_LIMIT),
        cost_estimate=pl.CostEstimate(
            flops=4 * rows * n * depth * pairs, bytes_accessed=2 * n * depth * (high + pairs) + 8 * rows * pairs, transcendentals=0
        ),
        name="product",
    )(start, *a_parts, *arrays, pos, *(() if first else sums))


def shift(value, axis, by):
    n = lax.axis_size(axis)
    return lax.ppermute(value, axis, [(i, (i + by) % n) for i in range(n)])


def together(*values):
    return lax.optimization_barrier(values)


def dense(integrals, amplitudes, tile_pattern, pair_domain, tile_order):
    count = tile_order.shape[0]
    placed = (tile_order[:, None] == jnp.arange(count, dtype=I32)[None, :]).astype(F32)
    exact = functools.partial(jnp.dot, precision=lax.Precision.HIGHEST)
    pattern = exact(exact(placed, tile_pattern.astype(F32)), placed.T)
    domain = exact(placed, pair_domain.astype(F32))
    here = count // (lax.axis_size(ROW))
    pattern = lax.dynamic_slice_in_dim(pattern, lax.axis_index(ROW) * here, here, 0)
    mask = jnp.repeat(jnp.repeat(pattern, TILE, axis=0), TILE, axis=1).astype(BF16)
    screened = lax.all_gather(integrals, COL, axis=1, tiled=True) * mask
    domain = jnp.repeat(domain, TILE, axis=0).astype(BF16)
    restricted = lax.all_gather(amplitudes, ROW, axis=0, tiled=True) * domain
    return jnp.dot(screened, restricted, preferred_element_type=F32)


def on_device(integrals, amplitudes, tile_pattern, pair_domain, tile_order):
    tall = amplitudes.shape[0] // TILE
    slots = amplitudes.shape[1] * tall * 5 // 9 // TILE * TILE
    recv = shift(integrals, "core", 1)
    pos, start, u, over = pack(pair_domain, amplitudes, tile_order, tall, slots, integrals.shape[1] // 2)
    mine = join(integrals, recv, over, tile_pattern, tile_order, tall)

    up, um = shift(u, "x", -1), shift(u, "x", 1)
    ap, am, there = shift(mine, "y", -1), shift(mine, "y", 1), shift(mine, "zl", 1)
    up, um, ap, am, there = together(up, um, ap, am, there)
    u2, q = shift(um, "x", 1), shift(u, "zh", 1)
    tp, tm = shift(there, "y", -1), shift(there, "y", 1)
    qp, qm, q2 = shift(q, "x", -1), shift(q, "x", 1), shift(u2, "zh", 1)
    a2, t2 = shift(am, "y", 1), shift(tp, "y", -1)

    arrays = [u, up, u2, um]
    early, late = ((0, 0), (0, 1), (0, 3)), ((0, 2), (1, 0), (1, 1), (1, 2), (1, 3))
    sums = product(start, early, (0, 1, 3), [mine, ap, am, there, tp, tm], arrays + [q] * 4, pos, tall)
    arrays += [q, qp, q2, qm]
    a_parts = [mine, ap, a2, am, there, tp, t2, tm]
    other, own, flags = product(start, late, (0, 1, 2, 3), a_parts, arrays, pos, tall, sums)
    theirs = shift(other, "core", 1)
    return lax.cond(
        jnp.max(flags) > 0.5,
        lambda *args: dense(*args[:5]),
        lambda *args: args[5] + args[6],
        integrals,
        amplitudes,
        tile_pattern,
        pair_domain,
        tile_order,
        own,
        theirs,
    )


def solution(mesh):
    fine = Mesh(np.asarray(mesh.devices).reshape(SIZES), AXES)
    return jax.shard_map(
        on_device,
        mesh=fine,
        in_specs=(P(ROW, COL), P(ROW, COL), P(), P(None, COL), P()),
        out_specs=P(ROW, COL),
        check_vma=False,
    )
```

```python
import functools

import jax
import jax.numpy as jnp
import numpy as np
from jax import lax
from jax.experimental import pallas as pl
from jax.experimental.pallas import tpu as pltpu
from jax.sharding import Mesh, PartitionSpec as P

TILE = 128
AXES = ("zh", "x", "core", "zl", "y")
SIZES = (2, 4, 2, 2, 4)
ROW, COL = ("zh", "x", "core"), ("zl", "y")
BF16, F32, I32 = jnp.bfloat16, jnp.float32, jnp.int32
FLAG_ROWS = 8
VMEM_LIMIT, LAST_LIMIT = 255 << 18, 60 << 20


def where_am_i():
    row = (lax.axis_index("zh") * 4 + lax.axis_index("x")) * 2 + lax.axis_index("core")
    return row, lax.axis_index("zl") * 4 + lax.axis_index("y"), lax.axis_index("core")


def iota(shape, dim):
    return lax.broadcasted_iota(I32, shape, dim)


def whole(n, space=pltpu.VMEM):
    return [pl.BlockSpec(memory_space=space)] * n


def join_kernel(tall, order, pattern, over_ref, a_ref, recv_ref, join_ref):
    row, col, core = where_am_i()
    rows, cols = a_ref.shape
    half = cols // TILE // 2
    for which, ref in ((1, recv_ref), (0, a_ref)):
        block = jnp.bitwise_xor(row, which)
        for i in range(rows // TILE):
            high = pl.ds(i * TILE, TILE)
            for j in range(half):
                tile = core * half + j
                on = pattern[order[block * tall + i], order[col * 2 * half + tile]]
                scale = on.astype(F32).astype(BF16)
                part = ref[high, pl.ds(pl.multiple_of(tile * TILE, TILE), TILE)]
                join_ref[pl.ds((1 - which) * rows + i * TILE, TILE), pl.ds(j * TILE, TILE)] = part * scale
    join_ref[pl.ds(2 * rows, FLAG_ROWS), :] = over_ref[...]


def join(integrals, recv, over, tile_pattern, tile_order, tall):
    rows, cols = integrals.shape
    return pl.pallas_call(
        functools.partial(join_kernel, tall),
        grid_spec=pltpu.PrefetchScalarGridSpec(
            num_scalar_prefetch=2, grid=(), in_specs=whole(3), out_specs=pl.BlockSpec(memory_space=pltpu.VMEM)
        ),
        out_shape=jax.ShapeDtypeStruct((2 * rows + FLAG_ROWS, cols // 2), BF16),
        compiler_params=pltpu.CompilerParams(vmem_limit_bytes=VMEM_LIMIT),
        name="join",
    )(tile_order, tile_pattern, over, integrals, recv)


def number(tall, dom, pos_ref, start_ref, started=None):
    tiles, pairs = dom.shape
    live = dom[...].astype(F32).astype(BF16)
    blocks = pairs // TILE
    spread = (iota((pairs, TILE), 0) // TILE == iota((pairs, TILE), 1)).astype(F32).astype(BF16)
    counts = jnp.dot(live, spread, preferred_element_type=F32)
    below = (iota((TILE, TILE), 0) < iota((TILE, TILE), 1)).astype(F32).astype(BF16)
    upto = (iota((TILE, TILE), 0) <= iota((TILE, TILE), 1)).astype(F32).astype(BF16)
    s0, s1 = iota((tiles, tiles), 0), iota((tiles, tiles), 1)
    before = ((s0 // tall == s1 // tall) & (s1 < s0)).astype(F32).astype(BF16)
    counted = counts.astype(BF16)
    ahead = jnp.sum(jnp.dot(before, counted, preferred_element_type=F32), axis=1, keepdims=True)
    starts = jnp.dot(counted, below, preferred_element_type=F32) + ahead
    start_ref[...] = starts.astype(I32)
    if started is not None:
        started.start()
    for b in range(blocks):
        lanes = pl.ds(b * TILE, TILE)
        here = live[:, b * TILE : (b + 1) * TILE]
        slot = jnp.dot(here, upto, preferred_element_type=F32) + (starts[:, b : b + 1] - 1.0)
        pos_ref[:, lanes] = jnp.where(dom[:, lanes] > 0, slot.astype(I32), -1)


def plan_kernel(tall, order, d_ref, pos_ref, start_ref, dom):
    for s in range(dom.shape[0]):
        dom[pl.ds(s, 1), :] = d_ref[pl.ds(order[s], 1), :]
    number(tall, dom, pos_ref, start_ref)


def plan(pair_domain, tile_order, tall):
    tiles, pairs = pair_domain.shape
    return pl.pallas_call(
        functools.partial(plan_kernel, tall),
        grid_spec=pltpu.PrefetchScalarGridSpec(
            num_scalar_prefetch=1,
            grid=(),
            in_specs=whole(1),
            out_specs=whole(2),
            scratch_shapes=[pltpu.VMEM((tiles, pairs), I32)],
        ),
        out_shape=[jax.ShapeDtypeStruct((tiles, pairs), I32), jax.ShapeDtypeStruct((tiles, TILE), I32)],
        compiler_params=pltpu.CompilerParams(vmem_limit_bytes=VMEM_LIMIT),
        cost_estimate=pl.CostEstimate(flops=0, bytes_accessed=4_000_000, transcendentals=0),
        name="plan",
    )(tile_order, pair_domain)


def pack_kernel(tall, slots, order, d_ref, b_ref, u_ref, over_ref, dom, pos, held, total, start, sem):
    tiles, pairs = d_ref.shape
    row = where_am_i()[0]
    dom[...] = jnp.zeros_like(dom)
    for i in range(tall):
        dom[pl.ds(i, 1), :] = d_ref[pl.ds(order[row * tall + i], 1), :]
    copy = pltpu.make_async_copy(held, start, sem)
    number(tall, dom, pos, held, copy)
    most = jnp.zeros((1, 1), I32)
    for s in range(0, tiles, tall):
        line = sum(d_ref[pl.ds(order[s + i], 1), :] for i in range(tall))
        most = jnp.maximum(most, jnp.sum(line, axis=1, keepdims=True))
    flag = jnp.where(most > slots, 1.0, 0.0).astype(F32)
    over_ref[...] = jnp.broadcast_to(flag, over_ref.shape).astype(BF16)
    total[...] = jnp.zeros_like(total)
    copy.wait()
    for i in range(tall):
        slot = pos[pl.ds(i, 1), :]
        for b in range(pairs // TILE):
            lanes = pl.ds(b * TILE, TILE)
            at = jnp.minimum(start[i, b] // TILE * TILE, slots)
            at = pl.multiple_of(at, TILE)
            pick = (iota((2 * TILE, TILE), 0) + at == slot[:, b * TILE : (b + 1) * TILE]).astype(F32).astype(BF16)
            moved = lax.dot_general(
                b_ref[pl.ds(i * TILE, TILE), lanes], pick, (((1,), (1,)), ((), ())), preferred_element_type=F32
            )
            total[:, pl.ds(at, 2 * TILE)] += moved
    u_ref[...] = total[:, :slots].astype(BF16)


def pack(pair_domain, amplitudes, tile_order, tall, slots, cols):
    tiles, pairs = pair_domain.shape
    return pl.pallas_call(
        functools.partial(pack_kernel, tall, slots),
        grid_spec=pltpu.PrefetchScalarGridSpec(
            num_scalar_prefetch=1,
            grid=(),
            in_specs=whole(2),
            out_specs=whole(2),
            scratch_shapes=[
                pltpu.VMEM((8, pairs), I32),
                pltpu.VMEM((8, pairs), I32),
                pltpu.VMEM((8, TILE), I32),
                pltpu.VMEM((TILE, slots + 2 * TILE), F32),
                pltpu.SMEM((8, TILE), I32),
                pltpu.SemaphoreType.DMA(()),
            ],
        ),
        out_shape=[jax.ShapeDtypeStruct((TILE, slots), BF16), jax.ShapeDtypeStruct((FLAG_ROWS, cols), BF16)],
        compiler_params=pltpu.CompilerParams(vmem_limit_bytes=VMEM_LIMIT),
        name="pack",
    )(tile_order, pair_domain, amplitudes)


def product_kernel(tall, picks, hops, first, wide, start_ref, *refs):
    n, nh = len(picks), len(hops)
    a_refs, refs = refs[: 2 * nh], refs[2 * nh :]
    in_refs, pos_ref, refs = refs[:8], refs[8], refs[9:]
    if not first:
        sums, flags_ref, refs = refs[:2], refs[2], refs[3:]
    outs, flag_out, (a_all, held, b_all, held_sums, start, a_sem, sem, in_sem, out_sem, start_sem) = refs[:2], refs[2], refs[3:]
    rows, pairs = outs[0].shape
    slots = in_refs[0].shape[1]
    depth = tall * TILE
    zh, x, core, zl, y = (lax.axis_index(axis) for axis in AXES)
    starts = pltpu.make_async_copy(start_ref, start, start_sem)
    starts.start()

    def a_slot(k):
        return a_all.at[:, pl.ds(k * depth, depth)]

    def b_slot(k):
        return held.at[k, :, pl.ds(0, slots)]

    ids = []
    for k, (dz, hop) in enumerate(picks):
        across, far = (y + hop) % 4, zh if dz == 0 else 1 - zh
        ids.append((far * 4 + across) * 2 + core)
        for dx in range(4):

            @pl.when((across - x + 4) % 4 == dx)
            def _(k=k, option=in_refs[4 * dz + dx]):
                pltpu.make_async_copy(option, b_slot(k), sem.at[k]).start()

        for own in range(2):

            @pl.when((far == zl) == (own == 0))
            def _(k=k, option=a_refs[own * nh + hops.index(hop)]):
                pltpu.make_async_copy(option, a_slot(k), a_sem.at[k]).start()

    strips = pairs // wide

    def strip(b):
        return pl.ds(b * wide, wide)

    if not first:
        loads = [
            [pltpu.make_async_copy(sums[h].at[:, strip(b)], held_sums.at[h, :, strip(b)], in_sem.at[h, b]) for h in range(2)]
            for b in range(strips)
        ]
        for pair in loads:
            for load in pair:
                load.start()
    for k in range(n):
        held[k, :, pl.ds(slots, TILE)] = jnp.zeros((TILE, TILE), BF16)

    lines = iota((2 * TILE, TILE), 0).astype(F32).astype(BF16)
    stores = []
    starts.wait()
    for b in range(strips):
        for k in range(n):
            if b == 0:
                pltpu.make_async_copy(in_refs[0], b_slot(k), sem.at[k]).wait()
            for i in range(tall):
                s = ids[k] * tall + i
                slot = pos_ref[pl.ds(s, 1), :]
                for c in range(wide // TILE):
                    block = b * (wide // TILE) + c
                    at = jnp.minimum(start[s, block] // TILE * TILE, slots - TILE)
                    at = pl.multiple_of(at, TILE)
                    here = slot[:, block * TILE : (block + 1) * TILE] - at
                    here = jnp.where((here < 0) | (here >= 2 * TILE), -1, here).astype(F32).astype(BF16)
                    pick = jnp.where(lines == here, jnp.ones((), BF16), jnp.zeros((), BF16))
                    spread = jnp.dot(held[k, :, pl.ds(at, 2 * TILE)], pick, preferred_element_type=F32)
                    b_all[pl.ds((k * tall + i) * TILE, TILE), pl.ds(c * TILE, TILE)] = spread.astype(BF16)
        if b == 0:
            for k in range(n):
                pltpu.make_async_copy(a_refs[0], a_slot(k), a_sem.at[k]).wait()
        for h in range(2):
            total = jnp.dot(a_all[pl.ds(h * rows, rows), :], b_all[...], preferred_element_type=F32)
            if not first:
                loads[b][h].wait()
                total += held_sums[h, :, strip(b)]
            held_sums[h, :, strip(b)] = total
            store = pltpu.make_async_copy(held_sums.at[h, :, strip(b)], outs[h].at[:, strip(b)], out_sem.at[h, b])
            store.start()
            stores.append(store)
    flags = [a_all[pl.ds(2 * rows, FLAG_ROWS), pl.ds(k * depth, TILE)].astype(F32) for k in range(n)]
    if not first:
        flags.append(flags_ref[...])
    flag_out[...] = functools.reduce(jnp.maximum, flags)
    for store in stores:
        store.wait()


def product(start, picks, hops, a_parts, arrays, pos, tall, sums=None, wide=1536):
    n, (tiles, pairs) = len(picks), pos.shape
    slots = arrays[0].shape[1]
    depth = tall * TILE
    high = a_parts[0].shape[0]
    rows = (high - FLAG_ROWS) // 2
    first = sums is None
    strips = pairs // wide
    hbm = pl.BlockSpec(memory_space=pltpu.HBM)
    vmem = pl.BlockSpec(memory_space=pltpu.VMEM)
    return pl.pallas_call(
        functools.partial(product_kernel, tall, picks, hops, first, wide),
        grid_spec=pltpu.PrefetchScalarGridSpec(
            num_scalar_prefetch=0,
            grid=(),
            in_specs=[hbm] * (len(a_parts) + 9) + [vmem] + ([] if first else [hbm, hbm, vmem]),
            out_specs=[hbm, hbm, vmem],
            scratch_shapes=[
                pltpu.VMEM((high, n * depth), BF16),
                pltpu.VMEM((n, TILE, slots + TILE), BF16),
                pltpu.VMEM((n * depth, wide), BF16),
                pltpu.VMEM((2, rows, pairs), F32),
                pltpu.SMEM((tiles, TILE), I32),
                pltpu.SemaphoreType.DMA((n,)),
                pltpu.SemaphoreType.DMA((n,)),
                pltpu.SemaphoreType.DMA((2, strips)),
                pltpu.SemaphoreType.DMA((2, strips)),
                pltpu.SemaphoreType.DMA(()),
            ],
        ),
        out_shape=[jax.ShapeDtypeStruct((rows, pairs), F32)] * 2 + [jax.ShapeDtypeStruct((FLAG_ROWS, TILE), F32)],
        compiler_params=pltpu.CompilerParams(vmem_limit_bytes=VMEM_LIMIT if first else LAST_LIMIT),
        cost_estimate=pl.CostEstimate(
            flops=4 * rows * n * depth * pairs, bytes_accessed=2 * n * depth * (high + pairs) + 8 * rows * pairs, transcendentals=0
        ),
        name="product",
    )(start, *a_parts, *arrays, pos, *(() if first else sums))


def shift(value, axis, by):
    n = lax.axis_size(axis)
    return lax.ppermute(value, axis, [(i, (i + by) % n) for i in range(n)])


def together(*values):
    return lax.optimization_barrier(values)


def dense(integrals, amplitudes, tile_pattern, pair_domain, tile_order):
    count = tile_order.shape[0]
    placed = (tile_order[:, None] == jnp.arange(count, dtype=I32)[None, :]).astype(F32)
    exact = functools.partial(jnp.dot, precision=lax.Precision.HIGHEST)
    pattern = exact(exact(placed, tile_pattern.astype(F32)), placed.T)
    domain = exact(placed, pair_domain.astype(F32))
    here = count // (lax.axis_size(ROW))
    pattern = lax.dynamic_slice_in_dim(pattern, lax.axis_index(ROW) * here, here, 0)
    mask = jnp.repeat(jnp.repeat(pattern, TILE, axis=0), TILE, axis=1).astype(BF16)
    screened = lax.all_gather(integrals, COL, axis=1, tiled=True) * mask
    domain = jnp.repeat(domain, TILE, axis=0).astype(BF16)
    restricted = lax.all_gather(amplitudes, ROW, axis=0, tiled=True) * domain
    return jnp.dot(screened, restricted, preferred_element_type=F32)


def on_device(integrals, amplitudes, tile_pattern, pair_domain, tile_order):
    tall = amplitudes.shape[0] // TILE
    slots = amplitudes.shape[1] * tall * 5 // 9 // TILE * TILE
    recv = shift(integrals, "core", 1)
    u, over = pack(pair_domain, amplitudes, tile_order, tall, slots, integrals.shape[1] // 2)
    mine = join(integrals, recv, over, tile_pattern, tile_order, tall)

    up, um = shift(u, "x", -1), shift(u, "x", 1)
    ap, am, there = shift(mine, "y", -1), shift(mine, "y", 1), shift(mine, "zl", 1)
    late_domain, _ = together(pair_domain, mine)
    pos, start = plan(late_domain, tile_order, tall)
    up, um, ap, am, there, pos, start = together(up, um, ap, am, there, pos, start)
    u2, q = shift(um, "x", 1), shift(u, "zh", 1)
    tp, tm = shift(there, "y", -1), shift(there, "y", 1)
    qp, qm, q2 = shift(q, "x", -1), shift(q, "x", 1), shift(u2, "zh", 1)
    a2, t2 = shift(am, "y", 1), shift(tp, "y", -1)

    arrays = [u, up, u2, um]
    early, late = ((0, 0), (0, 1), (0, 3)), ((0, 2), (1, 0), (1, 1), (1, 2), (1, 3))
    sums = product(start, early, (0, 1, 3), [mine, ap, am, there, tp, tm], arrays + [q] * 4, pos, tall)
    arrays += [q, qp, q2, qm]
    a_parts = [mine, ap, a2, am, there, tp, t2, tm]
    other, own, flags = product(start, late, (0, 1, 2, 3), a_parts, arrays, pos, tall, sums)
    theirs = shift(other, "core", 1)
    return lax.cond(
        jnp.max(flags) > 0.5,
        lambda *args: dense(*args[:5]),
        lambda *args: args[5] + args[6],
        integrals,
        amplitudes,
        tile_pattern,
        pair_domain,
        tile_order,
        own,
        theirs,
    )


def solution(mesh):
    fine = Mesh(np.asarray(mesh.devices).reshape(SIZES), AXES)
    return jax.shard_map(
        on_device,
        mesh=fine,
        in_specs=(P(ROW, COL), P(ROW, COL), P(), P(None, COL), P()),
        out_specs=P(ROW, COL),
        check_vma=False,
    )
```
